256 devices in a mesh: group: 8 (over z), mp: 32 (over y, x, core).
Axes of the slice: x: 4, y: 4, z: 8, core: 2. Of those that a mesh axis runs over, the one named last changes fastest.
Arguments:
- tokens: bfloat16 [256, 4, 8192], P(('group', 'mp')), may hold values from -6 to 6
- input_norm_gain: bfloat16 [8192], replicated, may hold values from 0.099609375 to 1.8984375
- query_weight: bfloat16 [8192, 4096], P(None, 'mp'), may hold values from -0.0625 to 0.0625
- key_value_weight: bfloat16 [8192, 1024], P('mp'), may hold values from -0.1875 to 0.1875
- output_weight: bfloat16 [4096, 8192], P('mp'), may hold values from -0.5 to 0.5
- stored_keys: bfloat16 [256, 4, 1024, 128], P(('group', 'mp')), may hold values from -384 to 384
- stored_values: bfloat16 [256, 4, 1024, 128], P(('group', 'mp')), may hold values from -6 to 6
- lengths: int32 [256], P(('group', 'mp')), may hold values from 1 to 1024, 131072 in all
- row_adapter: int32 [256], P('group'), may hold values from 0 to 255, as said below
- adapter_down: bfloat16 [256, 64, 8192], P('group', None, 'mp'), may hold values from -0.0625 to 0.0625
- adapter_up: bfloat16 [256, 64, 4096], P('group', None, 'mp'), may hold values from -0.75 to 0.75
Outputs:
- updated: bfloat16 [256, 4, 8192], P(('group', 'mp'))
The draws below stay inside these ranges and needn't reach their ends.
Inputs may be any that keep to these rules, and one draw needn't show every extreme that they name: `row_adapter`: adapter a is owned by group a // 32. Of the 32 rows of one group at most 8 use adapters of one owner group, and in every draw some owner group receives exactly 8 rows from every group.
All inputs are finite; a program needn't handle non-finite values. No bound on the sum of `lengths` on one device may be relied on, other than what follows from the above.
Results may differ from the reference program's by a relative error of at most 0.033.
Values may be sent and summed in bfloat16 or wider, within the bound.
No kernel may reach another device: no remote copies, remote signals or barrier semaphores. Data moves between devices by JAX's collectives and lax.ppermute only.
A program may use at most 64 MiB of HBM per device.

```python
import math
import jax
import jax.numpy as jnp
import numpy as np
from jax import lax

MODEL_WIDTH = 8192
HEAD_DIM = 128
ADAPTER_RANK = 64
DECODE_STEPS = 4
CTX = 1024
ADP_GROUP = 32
HEADS = 32
KV_HEADS = 4
QUERY_WIDTH = 4096
GROUP_ROWS = 32
REQUEST_ROWS = 256
CAP = 8
GROUPS = 8
ADAPTER_COUNT = 256


def draw_stored_keys(key, part):
    base_key = jax.random.fold_in(key, 0)
    values = jnp.clip(jax.random.normal(base_key, (REQUEST_ROWS, KV_HEADS, CTX, HEAD_DIM), jnp.float32), -6.0, 6.0)
    return values.astype(jnp.bfloat16)


def draw_row_adapter(key, part):
    busiest_key, rest_key = jax.random.split(key)
    busiest = jax.random.randint(busiest_key, (), 0, GROUPS)

    def one_group(group_key):
        pool_key, order_key, local_key = jax.random.split(group_key, 3)
        others = (busiest + 1 + jnp.arange((GROUPS - 1) * CAP) // CAP) % GROUPS
        chosen = jax.random.permutation(pool_key, others)[:GROUP_ROWS - CAP].astype(jnp.int32)
        owners = jnp.concatenate([jnp.full((CAP,), busiest, jnp.int32), chosen])
        owners = jax.random.permutation(order_key, owners)
        local_slot = jax.random.randint(local_key, (GROUP_ROWS,), 0, ADP_GROUP)
        return owners * ADP_GROUP + local_slot
    group_keys = jax.random.split(rest_key, GROUPS)
    return jax.vmap(one_group)(group_keys).reshape(REQUEST_ROWS).astype(jnp.int32)


def shard_levels(key, extent, pieces, least, high):
    level, own = 1.0, jax.random.fold_in(key, 6)
    for position, blocks in pieces:
        steps = jnp.exp(jax.random.uniform(jax.random.fold_in(own, position), (blocks,), jnp.float32, least / len(pieces), high / len(pieces)))
        level = level * jnp.repeat(steps, extent[position] // blocks).reshape([-1 if axis == position else 1 for axis in range(len(extent))])
    return level


def length_profile(amount, total, most, skew):
    weights = [(1 << 20) // math.isqrt(rank ** skew) + 1 for rank in range(2, amount + 1)]
    spare, holding = total - most - (amount - 1), [1] * (amount - 1)
    while spare > 0:
        candidates = [i for i in range(amount - 1) if holding[i] < most]
        mass, budget = sum([weights[i] for i in candidates]), spare
        for i in candidates:
            addition = min(most - holding[i], max(1, budget * weights[i] // mass), spare)
            holding[i] = holding[i] + addition
            spare = spare - addition
    return np.array([most] + holding)


def ragged_sizes(rng, count, total, reach, lean):
    if count == 2:
        one = jax.random.randint(rng, (), max(1, total - reach), min(reach, total - 1) + 1)
        return jnp.stack([one, total - one])
    tallies = jnp.asarray(length_profile(count, total, reach, lean), jnp.int32)
    twos = (count - 1) // 2
    donor, taker = tallies[1:1 + 2 * twos:2], tallies[2:2 + 2 * twos:2]
    room = jnp.minimum(donor - 1, reach - taker)
    shifted = jax.random.randint(jax.random.fold_in(rng, 1), (twos,), 0, 1 << 20) % (room + 1)
    tallies = tallies.at[1:1 + 2 * twos:2].set(donor - shifted).at[2:2 + 2 * twos:2].set(taker + shifted)
    return tallies[jax.random.permutation(jax.random.fold_in(rng, 2), count)]


def gaussian(stream_key, shape, scale, limit, shards=(), dtype=jnp.bfloat16):
    array = jax.random.normal(stream_key, shape, jnp.float32) * scale
    if len(shards) > 0:
        array = shard_levels(stream_key, shape, shards, -0.22, 0.18) * array
    return jnp.clip(array, min=-limit, max=limit).astype(dtype)


def setup_inputs(seed: int = 0) -> dict:
    key_list = jax.random.split(jax.random.key(seed), 12)
    return {
        "tokens": gaussian(key_list[0], (REQUEST_ROWS, DECODE_STEPS, MODEL_WIDTH), 1.0, 6.0, ((0, 256),)),
        "input_norm_gain": jnp.clip(1.0 + 0.18 * jax.random.normal(key_list[1], (MODEL_WIDTH,), jnp.float32), 0.099609375, 1.8984375).astype(jnp.bfloat16),
        "query_weight": gaussian(key_list[2], (MODEL_WIDTH, QUERY_WIDTH), MODEL_WIDTH ** -0.5, 0.0625, ((1, 32),)),
        "key_value_weight": gaussian(key_list[3], (MODEL_WIDTH, 2 * KV_HEADS * HEAD_DIM), (MODEL_WIDTH // 8) ** -0.5, 0.1875, ((0, 32),)),
        "output_weight": gaussian(key_list[4], (QUERY_WIDTH, MODEL_WIDTH), HEAD_DIM ** -0.5, 0.5, ((0, 32),)),
        "stored_keys": draw_stored_keys(jax.random.fold_in(key_list[11], 71), 0),
        "stored_values": gaussian(key_list[6], (REQUEST_ROWS, KV_HEADS, CTX, HEAD_DIM), 1.0, 6.0, ((0, 256),)),
        "lengths": ragged_sizes(key_list[7], REQUEST_ROWS, REQUEST_ROWS * CTX // 2, CTX, 2).astype(jnp.int32),
        "row_adapter": draw_row_adapter(jax.random.fold_in(key_list[11], 71), 0),
        "adapter_down": gaussian(key_list[9], (ADAPTER_COUNT, ADAPTER_RANK, MODEL_WIDTH), MODEL_WIDTH ** -0.5, 0.0625, ((0, 8), (2, 32))),
        "adapter_up": gaussian(key_list[10], (ADAPTER_COUNT, ADAPTER_RANK, QUERY_WIDTH), ADAPTER_RANK ** -0.5, 0.75, ((0, 8), (2, 32))),
    }


norm_eps = 1e-05
masked_score = -1e+30

def adapter_block(input_couple):
    normalized_share, adapter_share, adapter_down, adapter_up = input_couple
    down_selected = adapter_down[adapter_share].astype(jnp.float32)
    reduced_rank = jnp.einsum('rsd,rkd->rsk', normalized_share.astype(jnp.float32), down_selected).astype(jnp.bfloat16)
    up_selected = adapter_up[adapter_share].astype(jnp.float32)
    return jnp.einsum('nth,nhb->ntb', reduced_rank.astype(jnp.float32), up_selected).astype(jnp.bfloat16)

def attend_block(inputs_tuple):
    query_part, keys_part, values_part, fresh_part, length_part = inputs_tuple
    block_rows = query_part.shape[0]
    grouped_q = query_part.reshape(block_rows, DECODE_STEPS, KV_HEADS, HEADS // KV_HEADS, HEAD_DIM).astype(jnp.float32)
    scaling = HEAD_DIM ** (-0.5)
    cache_scores = jnp.einsum('rsgjh,rgch->rgjsc', grouped_q, keys_part.astype(jnp.float32)) * scaling
    cache_live = (jnp.arange(CTX)[None, :] < length_part[:, None])[:, None, None, None, :]
    cache_scores = jnp.where(cache_live, cache_scores, masked_score)
    fresh_keys = fresh_part[:, :, 0].astype(jnp.float32)
    fresh_values = fresh_part[:, :, 1].astype(jnp.float32)
    fresh_scores = jnp.einsum('rsgjh,rtgh->rgjst', grouped_q, fresh_keys) * scaling
    step_live = jnp.arange(DECODE_STEPS)[None, :] <= jnp.arange(DECODE_STEPS)[:, None]
    fresh_scores = jnp.where(step_live, fresh_scores, masked_score)
    largest = jnp.maximum(lax.optimization_barrier(jnp.max(cache_scores, axis=-1)), lax.optimization_barrier(jnp.max(fresh_scores, axis=-1)))[..., None]
    cache_exp = jnp.exp(cache_scores - largest)
    fresh_exp = jnp.exp(fresh_scores - largest)
    total = lax.optimization_barrier(jnp.sum(cache_exp, axis=-1, keepdims=True)) + lax.optimization_barrier(jnp.sum(fresh_exp, axis=-1, keepdims=True))
    cache_weights = (cache_exp / total).astype(jnp.bfloat16)
    fresh_weights = (fresh_exp / total).astype(jnp.bfloat16)
    attended = jnp.einsum('rgjsc,rgch->rsgjh', cache_weights.astype(jnp.float32), values_part.astype(jnp.float32))
    attended = attended + jnp.einsum('rgjst,rtgh->rsgjh', fresh_weights.astype(jnp.float32), fresh_values)
    return attended.astype(jnp.bfloat16).reshape(block_rows, DECODE_STEPS, QUERY_WIDTH)

def reference(tokens, input_norm_gain, query_weight, key_value_weight, output_weight, stored_keys, stored_values, lengths, row_adapter, adapter_down, adapter_up):
    widened = tokens.astype(jnp.float32)
    normalized = (widened * lax.rsqrt(lax.optimization_barrier(jnp.mean(widened * widened, axis=-1, keepdims=True)) + norm_eps) * input_norm_gain.astype(jnp.float32)).astype(jnp.bfloat16)
    flat_rows = normalized.reshape(REQUEST_ROWS * DECODE_STEPS, MODEL_WIDTH)
    query_plain = jnp.dot(flat_rows, query_weight, preferred_element_type=jnp.float32).reshape(REQUEST_ROWS, DECODE_STEPS, QUERY_WIDTH)
    fresh_kv = jnp.dot(flat_rows, key_value_weight, preferred_element_type=jnp.float32).astype(jnp.bfloat16)
    fresh_kv = fresh_kv.reshape(REQUEST_ROWS, DECODE_STEPS, 2, KV_HEADS, HEAD_DIM)
    count_blocks = REQUEST_ROWS // GROUP_ROWS

    def adapter_step(input_couple):
        return adapter_block((input_couple[0], input_couple[1], adapter_down, adapter_up))
    adapter_delta = lax.map(adapter_step, (normalized.reshape(count_blocks, GROUP_ROWS, DECODE_STEPS, MODEL_WIDTH), row_adapter.reshape(count_blocks, GROUP_ROWS)))
    adapter_delta = adapter_delta.reshape(REQUEST_ROWS, DECODE_STEPS, QUERY_WIDTH)
    query_rows = (query_plain + adapter_delta.astype(jnp.float32)).astype(jnp.bfloat16)
    attended = lax.map(attend_block, (query_rows.reshape(count_blocks, GROUP_ROWS, DECODE_STEPS, QUERY_WIDTH), stored_keys.reshape(count_blocks, GROUP_ROWS, KV_HEADS, CTX, HEAD_DIM), stored_values.reshape(count_blocks, GROUP_ROWS, KV_HEADS, CTX, HEAD_DIM), fresh_kv.reshape(count_blocks, GROUP_ROWS, DECODE_STEPS, 2, KV_HEADS, HEAD_DIM), lengths.reshape(count_blocks, GROUP_ROWS)))
    attended = attended.reshape(REQUEST_ROWS * DECODE_STEPS, QUERY_WIDTH)
    mixed = jnp.dot(attended, output_weight, preferred_element_type=jnp.float32).reshape(REQUEST_ROWS, DECODE_STEPS, MODEL_WIDTH)
    return (widened + mixed).astype(jnp.bfloat16)
```

```python
import jax
import jax.numpy as jnp
from jax import lax
from jax.sharding import PartitionSpec as P

norm_eps = 1e-05
masked_score = -1e30


def attend_rows(head_queries, stored_keys, stored_values, fresh_buffer, lengths):
    head_count, row_count, block_size, head_dim = head_queries.shape
    kv_heads = stored_keys.shape[1]
    context = stored_keys.shape[2]
    total_steps = fresh_buffer.shape[1]
    grouped_q = head_queries.reshape(
        kv_heads, head_count // kv_heads, row_count, block_size, head_dim
    )
    scaling = head_dim ** (-0.5)
    cache_scores = (
        jnp.einsum("gjrsh,rgch->rgjsc", grouped_q, stored_keys, preferred_element_type=jnp.float32)
        * scaling
    )
    cache_live = (jnp.arange(context)[None, :] < lengths[:, None])[:, None, None, None, :]
    cache_scores = jnp.where(cache_live, cache_scores, masked_score)
    fresh_split = fresh_buffer.reshape(row_count, total_steps, 2, kv_heads, head_dim)
    fresh_scores = (
        jnp.einsum(
            "gjrsh,rtgh->rgjst", grouped_q, fresh_split[:, :, 0], preferred_element_type=jnp.float32
        )
        * scaling
    )
    step_live = jnp.arange(total_steps)[None, :] <= jnp.arange(block_size)[:, None]
    fresh_scores = jnp.where(step_live, fresh_scores, masked_score)
    largest = jnp.maximum(jnp.max(cache_scores, axis=-1), jnp.max(fresh_scores, axis=-1))[..., None]
    cache_exp = jnp.exp(cache_scores - largest)
    fresh_exp = jnp.exp(fresh_scores - largest)
    total = jnp.sum(cache_exp, axis=-1, keepdims=True) + jnp.sum(fresh_exp, axis=-1, keepdims=True)
    cache_weights = (cache_exp / total).astype(jnp.bfloat16)
    fresh_weights = (fresh_exp / total).astype(jnp.bfloat16)
    attended = jnp.einsum(
        "rgjsc,rgch->gjrsh", cache_weights, stored_values, preferred_element_type=jnp.float32
    )
    attended = attended + jnp.einsum(
        "rgjst,rtgh->gjrsh", fresh_weights, fresh_split[:, :, 1], preferred_element_type=jnp.float32
    )
    return attended.astype(jnp.bfloat16).reshape(head_count, row_count, block_size, head_dim)


def swap_cores(value):
    size = lax.axis_size("mp")
    return lax.ppermute(value, "mp", [(i, i ^ 1) for i in range(size)])


def chip_groups(size):
    return [[2 * i + c for i in range(size // 2)] for c in range(2)]


def exchange(value, axis, groups=None):
    return lax.all_to_all(
        value, axis, split_axis=0, concat_axis=0, tiled=True, axis_index_groups=groups
    )


def gather_rows(value, core):
    size = lax.axis_size("mp")
    copies = jnp.broadcast_to(value, (size // 2,) + value.shape[1:])
    own = exchange(copies, "mp", chip_groups(size))
    other = swap_cores(own)
    first = jnp.where(core == 0, own, other)
    second = jnp.where(core == 0, other, own)
    return jnp.stack([first, second], axis=1).reshape((size,) + value.shape[1:])


def scatter_sum(partial, core):
    size = lax.axis_size("mp")
    pairs = partial.astype(jnp.bfloat16).reshape((size // 2, 2) + partial.shape[1:])
    kept = jnp.where(core == 0, pairs[:, 0], pairs[:, 1])
    given = jnp.where(core == 0, pairs[:, 1], pairs[:, 0])
    taken = swap_cores(given)
    both = (kept.astype(jnp.float32) + taken.astype(jnp.float32)).astype(jnp.bfloat16)
    return jnp.sum(
        exchange(both, "mp", chip_groups(size)).astype(jnp.float32), axis=0, keepdims=True
    )


def body(
    tokens,
    input_norm_gain,
    query_weight,
    key_value_weight,
    output_weight,
    stored_keys,
    stored_values,
    lengths,
    row_adapter,
    adapter_down,
    adapter_up,
):
    rows_dev, total_steps, width = tokens.shape
    mp_count = lax.axis_size("mp")
    group_count = lax.axis_size("group")
    mp_index = lax.axis_index("mp")
    core = mp_index % 2
    head_dim = query_weight.shape[1]
    slice_width = key_value_weight.shape[0]
    row_group = row_adapter.shape[0]
    capacity = row_group // 4
    adapter_group = adapter_down.shape[0]
    rank = adapter_down.shape[1]
    owner_group = row_adapter // adapter_group
    local_slot = row_adapter % adapter_group
    earlier = jnp.arange(row_group)[None, :] <= jnp.arange(row_group)[:, None]
    same_owner = owner_group[:, None] == owner_group[None, :]
    within_owner = jnp.sum((earlier & same_owner).astype(jnp.int32), axis=1) - 1
    destination = owner_group * capacity + within_owner
    slot_iota = jnp.arange(group_count * capacity)
    placement = slot_iota[:, None] == destination[None, :]
    place_matrix = placement.astype(jnp.bfloat16)
    slot_number = jnp.sum(jnp.where(placement, local_slot[None, :] + 1, 0), axis=1)
    slot_number = slot_number.reshape(group_count, capacity)
    widened = tokens.astype(jnp.float32)
    normalized = (
        widened
        * lax.rsqrt(jnp.mean(widened * widened, axis=-1, keepdims=True) + norm_eps)
        * input_norm_gain.astype(jnp.float32)
    ).astype(jnp.bfloat16)
    gathered = gather_rows(normalized, core)
    mine = lax.dynamic_slice_in_dim(gathered, mp_index * slice_width, slice_width, 2)
    sent_rows = jnp.einsum(
        "pr,rsd->psd", place_matrix, mine, preferred_element_type=jnp.float32
    ).astype(jnp.bfloat16)
    sent_rows = sent_rows.reshape(group_count, capacity * total_steps, slice_width)
    numbers = jnp.pad(
        slot_number.astype(jnp.bfloat16)[:, None, :],
        ((0, 0), (0, 0), (0, slice_width - capacity)),
    )
    received = exchange(jnp.concatenate([sent_rows, numbers], axis=1), "group")
    received_rows = received[:, : capacity * total_steps].reshape(
        group_count, capacity, total_steps, slice_width
    )
    adapter_slot = received[:, capacity * total_steps, :capacity].astype(jnp.int32) - 1
    query_plain = jnp.einsum(
        "rsd,dh->rsh", gathered, query_weight, preferred_element_type=jnp.float32
    )
    fresh_partial = jnp.einsum(
        "rsd,dk->rsk", mine, key_value_weight, preferred_element_type=jnp.float32
    ).astype(jnp.bfloat16)
    valid_slot = adapter_slot >= 0
    clamped_slot = jnp.where(valid_slot, adapter_slot, 0)
    partial_rank = jnp.einsum(
        "ljon,ljmn->ljom",
        received_rows,
        adapter_down[clamped_slot],
        preferred_element_type=jnp.float32,
    )
    partial_rank = jnp.where(valid_slot[:, :, None, None], partial_rank, 0.0)
    shares = partial_rank.reshape(mp_count, -1, total_steps, rank)
    summed = jnp.sum(exchange(shares, "mp"), axis=0).astype(jnp.bfloat16)
    rank_entries = exchange(jnp.broadcast_to(summed[None], shares.shape), "mp").reshape(
        group_count, capacity, total_steps, rank
    )
    slot_delta = jnp.einsum(
        "ljiw,ljwq->ljiq",
        rank_entries,
        adapter_up[clamped_slot],
        preferred_element_type=jnp.float32,
    ).astype(jnp.bfloat16)
    returned = exchange(slot_delta, "group").reshape(
        group_count * capacity, total_steps, head_dim
    )
    adapter_delta = jnp.einsum(
        "pr,psh->rsh", place_matrix, returned, preferred_element_type=jnp.float32
    )
    query_rows = (query_plain + adapter_delta).astype(jnp.bfloat16)
    arrived = exchange(jnp.concatenate([query_rows, fresh_partial], axis=2), "mp")
    head_queries = arrived[:, None, :, :head_dim]
    fresh_buffer = jnp.sum(
        arrived[:, :, head_dim:].astype(jnp.float32), axis=0, keepdims=True
    ).astype(jnp.bfloat16)
    attended = attend_rows(head_queries, stored_keys, stored_values, fresh_buffer, lengths)
    head_rows = exchange(attended, "mp").reshape(row_group, total_steps, head_dim)
    mixed = scatter_sum(
        jnp.einsum("rsh,hd->rsd", head_rows, output_weight, preferred_element_type=jnp.float32),
        core,
    )
    return (widened + mixed).astype(jnp.bfloat16)


def solution(mesh):
    return jax.shard_map(
        body,
        mesh=mesh,
        in_specs=(
            P(("group", "mp"), None, None),
            P(),
            P(None, "mp"),
            P("mp", None),
            P("mp", None),
            P(("group", "mp"), None, None, None),
            P(("group", "mp"), None, None, None),
            P(("group", "mp")),
            P("group"),
            P("group", None, "mp"),
            P("group", None, "mp"),
        ),
        out_specs=P(("group", "mp"), None, None),
        check_vma=False,
    )
```
